32 devices in a mesh: narrow: 4 (over z), wide: 8 (over y, x, core).
Axes of the slice: x: 2, y: 2, z: 4, core: 2. Of those that a mesh axis runs over, the one named last changes fastest.
Arguments:
- hidden_in: bfloat16 [8, 2048, 2048], P('narrow', 'wide'), may hold values from -6 to 6
- out_grad: bfloat16 [8, 2048, 2048], P('narrow', 'wide'), may hold values from -6 to 6
- doc_lengths: int32 [8, 8], P('narrow'), may hold values from 1 to 1024, 2048 in all within a row
- attn_gain: bfloat16 [2048], P('narrow'), may hold values from 0.5 to 1.5
- w_query: bfloat16 [2048, 2048], P('narrow', 'wide'), may hold values from -0.125 to 0.125
- w_key: bfloat16 [2048, 2048], P('narrow', 'wide'), may hold values from -0.125 to 0.125
- w_value: bfloat16 [2048, 2048], P('narrow', 'wide'), may hold values from -0.125 to 0.125
- w_out: bfloat16 [2048, 2048], P('wide', 'narrow'), may hold values from -1 to 1
- mlp_gain: bfloat16 [2048], P('narrow'), may hold values from 0.5 to 1.5
- w_gate: bfloat16 [2048, 8192], P('narrow', 'wide'), may hold values from -0.125 to 0.125
- w_up: bfloat16 [2048, 8192], P('narrow', 'wide'), may hold values from -0.125 to 0.125
- w_down: bfloat16 [8192, 2048], P('wide', 'narrow'), may hold values from -0.0625 to 0.0625
Outputs:
- hidden_out: bfloat16 [8, 2048, 2048], P('narrow', 'wide')
- in_grad: bfloat16 [8, 2048, 2048], P('narrow', 'wide')
- grad_attn_gain: float32 [2048], P(('narrow', 'wide'))
- grad_w_query: float32 [2048, 2048], P('narrow', 'wide')
- grad_w_key: float32 [2048, 2048], P('narrow', 'wide')
- grad_w_value: float32 [2048, 2048], P('narrow', 'wide')
- grad_w_out: float32 [2048, 2048], P('wide', 'narrow')
- grad_mlp_gain: float32 [2048], P(('narrow', 'wide'))
- grad_w_gate: float32 [2048, 8192], P('narrow', 'wide')
- grad_w_up: float32 [2048, 8192], P('narrow', 'wide')
- grad_w_down: float32 [8192, 2048], P('wide', 'narrow')
The draws below stay inside these ranges and needn't reach their ends.
Inputs may be any that keep to these rules, and one draw needn't show every extreme that they name: `doc_lengths`: in every row the 8 lengths sum to 2048, and the longest is exactly 1024.
All inputs are finite; a program needn't handle non-finite values.
Results may differ from the reference program's by a relative error of at most 0.029.
Values may be sent and summed in bfloat16 or wider, within the bound.
No kernel may reach another device: no remote copies, remote signals or barrier semaphores. Data moves between devices by JAX's collectives and lax.ppermute only.
A program may use at most 192 MiB of HBM per device.

```python
import math
import jax
import jax.numpy as jnp
import numpy as np
from jax import lax

D = 2048
HEADS = 32
HEAD_DIM = 64
FF = 8192
SEQ = 2048
DOCS = 8
ROWS = 8
GROUPS = 8


def block_scale(rng, shape, pieces, least, top_value):
    factor_of = 1.0
    for axis_at, blocks in pieces:
        heights = jax.random.uniform(jax.random.fold_in(jax.random.fold_in(rng, 6), axis_at), (blocks,), jnp.float32, least / len(pieces), top_value / len(pieces))
        factor_of = factor_of * jnp.repeat(jnp.exp(heights), shape[axis_at] // blocks).reshape((-1,) + (1,) * (len(shape) - 1 - axis_at))
    return factor_of


def length_profile(amount, total, reach, skew):
    loads = [(1 << 20) // math.isqrt(standing ** skew) + 1 for standing in range(2, amount + 1)]
    surplus, given = total - reach - (amount - 1), [1] * (amount - 1)
    while surplus > 0:
        candidates = [i for i in range(amount - 1) if given[i] < reach]
        mass, budget = sum([loads[i] for i in candidates]), surplus
        for i in candidates:
            addition = min(reach - given[i], max(1, budget * loads[i] // mass), surplus)
            given[i] = given[i] + addition
            surplus = surplus - addition
    return np.array([reach] + given)


def uneven(stream_key, count, total, limit, slope):
    if count == 2:
        one = jax.random.randint(stream_key, (), max(1, total - limit), min(limit, total - 1) + 1)
        return jnp.stack([one, total - one])
    sizes = jnp.asarray(length_profile(count, total, limit, slope), jnp.int32)
    pairs = (count - 1) // 2
    source_of, taker = sizes[1:1 + 2 * pairs:2], sizes[2:2 + 2 * pairs:2]
    slack = jnp.minimum(source_of - 1, limit - taker)
    moved = jax.random.randint(jax.random.fold_in(stream_key, 1), (pairs,), 0, 1 << 20) % (slack + 1)
    sizes = sizes.at[1:1 + 2 * pairs:2].set(source_of - moved).at[2:2 + 2 * pairs:2].set(taker + moved)
    return sizes[jax.random.permutation(jax.random.fold_in(stream_key, 2), count)]


def normal_values(stream_key, shape, scale, bound, cuts=(), kind=jnp.bfloat16):
    values = jax.random.normal(stream_key, shape, jnp.float32) * scale
    if len(cuts) > 0:
        values = block_scale(stream_key, shape, cuts, -0.22, 0.18) * values
    return jnp.clip(values, min=-bound, max=bound).astype(kind)


def setup_inputs(seed: int = 0) -> dict:
    key_of = jax.random.split(jax.random.key(seed), 13)
    return {
        "hidden_in": normal_values(key_of[0], (ROWS, SEQ, D), 1.0, 6.0, ((0, 4), (1, 8))),
        "out_grad": normal_values(key_of[1], (ROWS, SEQ, D), 1.0, 6.0, ((0, 4), (1, 8))),
        "doc_lengths": jax.vmap(lambda own: uneven(own, DOCS, SEQ, SEQ // 2, 2))(jax.random.split(key_of[2], ROWS)).reshape((ROWS, DOCS)).astype(jnp.int32),
        "attn_gain": jnp.clip(1.0 + 0.1 * jax.random.normal(key_of[3], (D,), jnp.float32), 0.5, 1.5).astype(jnp.bfloat16),
        "w_query": normal_values(key_of[4], (D, D), D ** -0.5, 0.125, ((0, 4), (1, 8))),
        "w_key": normal_values(key_of[5], (D, D), D ** -0.5, 0.125, ((0, 4), (1, 8))),
        "w_value": normal_values(key_of[6], (D, D), D ** -0.5, 0.125, ((0, 4), (1, 8))),
        "w_out": normal_values(key_of[7], (D, D), (D // 64) ** -0.5, 1.0, ((0, 8), (1, 4))),
        "mlp_gain": jnp.clip(1.0 + 0.1 * jax.random.normal(key_of[8], (D,), jnp.float32), 0.5, 1.5).astype(jnp.bfloat16),
        "w_gate": normal_values(key_of[9], (D, FF), D ** -0.5, 0.125, ((0, 4), (1, 8))),
        "w_up": normal_values(key_of[10], (D, FF), D ** -0.5, 0.125, ((0, 4), (1, 8))),
        "w_down": normal_values(key_of[11], (FF, D), FF ** -0.5, 0.0625, ((0, 8), (1, 4))),
    }


EPS = 1e-05
NEG = -1e+30
ROPE_BASE = 130000.0
PRECISE = lax.Precision.HIGHEST

@jax.custom_vjp
def low(v):
    return lax.optimization_barrier(v.astype(jnp.bfloat16)).astype(jnp.float32)

@jax.custom_vjp
def low_back(v):
    return v

def low_keep(v):
    return (low(v), None)

def low_pass(kept, grad):
    return (grad,)

def back_keep(v):
    return (v, None)

def back_low(kept, grad):
    return (low(grad),)
low.defvjp(low_keep, low_pass)
low_back.defvjp(back_keep, back_low)

def mat_high(left_op, right_op):
    return jnp.dot(left_op, right_op, precision=PRECISE)

def doc_starts(lengths):
    tokens = jnp.arange(SEQ, dtype=jnp.int32)
    ends_at = jnp.cumsum(lengths).astype(jnp.int32)
    before = jnp.where(ends_at[None, :] <= tokens[:, None], ends_at[None, :], jnp.int32(0))
    return lax.optimization_barrier(jnp.max(before, axis=1)).astype(jnp.int32)

def rope_tables(starts):
    half_dim = HEAD_DIM // 2
    position = (jnp.arange(SEQ, dtype=jnp.int32) - starts).astype(jnp.float32)
    inverse = ROPE_BASE ** (-(jnp.arange(half_dim, dtype=jnp.float32) * 2.0) / HEAD_DIM)
    angles = position[:, None] * inverse[None, :]
    return (jnp.cos(angles)[:, None, :], jnp.sin(angles)[:, None, :])

def rotate(tensor, cos_table, sin_table):
    half_dim = tensor.shape[-1] // 2
    front_half = tensor[..., :half_dim]
    back_half = tensor[..., half_dim:]
    return jnp.concatenate([front_half * cos_table - back_half * sin_table, back_half * cos_table + front_half * sin_table], axis=-1)

def attention(queries, keys_rot, values_in, starts):
    block_len = min(512, SEQ)
    n_blocks = SEQ // block_len
    score_scale = HEAD_DIM ** (-0.5)
    blocks = queries.reshape(n_blocks, block_len, HEADS, HEAD_DIM)
    firsts = jnp.arange(n_blocks, dtype=jnp.int32) * block_len
    columns = jnp.arange(SEQ, dtype=jnp.int32)

    def one_block(block_pair):
        q_block, first_row = block_pair
        row_ids = first_row + jnp.arange(block_len, dtype=jnp.int32)
        begins = lax.dynamic_slice_in_dim(starts, first_row, block_len)
        allowed = (columns[None, :] <= row_ids[:, None]) & (columns[None, :] >= begins[:, None])
        scores = low_back(score_scale * jnp.einsum('qhd,khd->hqk', q_block, keys_rot, precision=PRECISE))
        masked = jnp.where(allowed[None], scores, NEG)
        row_max = lax.optimization_barrier(jnp.max(masked, axis=-1, keepdims=True))
        exp_terms = jnp.exp(masked - row_max)
        prob_rows = low(exp_terms / lax.optimization_barrier(jnp.sum(exp_terms, axis=-1, keepdims=True)))
        return jnp.einsum('hqk,khd->qhd', prob_rows, values_in, precision=PRECISE)
    block_outs = lax.map(jax.checkpoint(one_block), (blocks, firsts))
    return block_outs.reshape(SEQ, HEADS * HEAD_DIM)

def rms_scale(values_in):
    return values_in * lax.rsqrt(lax.optimization_barrier(jnp.mean(values_in * values_in, axis=-1, keepdims=True)) + EPS)

def layer(residual, params, starts, cos_table, sin_table):
    attn_gain, w_query, w_key, w_value, w_out, mlp_gain, w_gate, w_up, w_down = params
    head_width = D // GROUPS
    ff_width = FF // GROUPS
    group_shape = (SEQ, HEADS // GROUPS, HEAD_DIM)
    attn_in = low(rms_scale(residual) * attn_gain)
    query_parts, key_parts, value_parts = ([], [], [])
    for group in range(GROUPS):
        shared = low_back(attn_in)
        first_col = group * head_width
        last_col = first_col + head_width
        query_parts.append(low(rotate(low_back(mat_high(shared, w_query[:, first_col:last_col])).reshape(group_shape), cos_table, sin_table)))
        key_parts.append(low(rotate(low_back(mat_high(shared, w_key[:, first_col:last_col])).reshape(group_shape), cos_table, sin_table)))
        value_parts.append(low(low_back(mat_high(shared, w_value[:, first_col:last_col]))).reshape(group_shape))
    queries = jnp.concatenate(query_parts, axis=1)
    keys_rot = jnp.concatenate(key_parts, axis=1)
    values_in = jnp.concatenate(value_parts, axis=1)
    attended = low(low_back(attention(queries, keys_rot, values_in, starts)))
    attn_total = jnp.zeros((SEQ, D), jnp.float32)
    for group in range(GROUPS):
        first_col = group * head_width
        last_col = first_col + head_width
        attn_total = attn_total + low(mat_high(attended[:, first_col:last_col], w_out[first_col:last_col, :]))
    middle = residual + low_back(attn_total)
    mlp_in = low(rms_scale(middle) * mlp_gain)
    mlp_total = jnp.zeros((SEQ, D), jnp.float32)
    for group in range(GROUPS):
        shared = low_back(mlp_in)
        first_col = group * ff_width
        last_col = first_col + ff_width
        gate_pre = low_back(mat_high(shared, w_gate[:, first_col:last_col]))
        up_pre = low_back(mat_high(shared, w_up[:, first_col:last_col]))
        hidden = low(gate_pre * jax.nn.sigmoid(gate_pre) * up_pre)
        mlp_total = mlp_total + low(mat_high(hidden, w_down[first_col:last_col, :]))
    return middle + low_back(mlp_total)

def reference(hidden_in, out_grad, doc_lengths, attn_gain, w_query, w_key, w_value, w_out, mlp_gain, w_gate, w_up, w_down):
    params = tuple((weight.astype(jnp.float32) for weight in (attn_gain, w_query, w_key, w_value, w_out, mlp_gain, w_gate, w_up, w_down)))

    def per_row(totals, row_pack):
        input_row, grad_row, lengths = row_pack
        starts = doc_starts(lengths)
        cos_table, sin_table = rope_tables(starts)

        def forward(residual, weights):
            return layer(residual, weights, starts, cos_table, sin_table)
        result, pullback = jax.vjp(forward, input_row.astype(jnp.float32), params)
        grad_input, grad_params = pullback(grad_row.astype(jnp.float32))
        totals = tuple((summed + gradient for summed, gradient in zip(totals, grad_params)))
        return (totals, (result.astype(jnp.bfloat16), grad_input.astype(jnp.bfloat16)))
    zero_grads = tuple((jnp.zeros_like(weight) for weight in params))
    totals, (outputs, input_grads) = lax.scan(per_row, zero_grads, (hidden_in, out_grad, doc_lengths))
    return (outputs, input_grads, totals[0], totals[1], totals[2], totals[3], totals[4], totals[5], totals[6], totals[7], totals[8])
```

```python
import functools

import jax
import jax.numpy as jnp
from jax import lax
from jax.experimental import pallas as pl
from jax.experimental.pallas import tpu as pltpu
from jax.sharding import PartitionSpec as P

HEAD_DIM = 64
PAIR = 2 * HEAD_DIM
EPS = 1e-05
NEG = -1e30
ROPE_BASE = 130000.0
SCALE = HEAD_DIM ** (-0.5)


BF = jnp.bfloat16
F32 = jnp.float32
NN = (((1,), (0,)), ((), ()))
NT = (((1,), (1,)), ((), ()))
TN = (((0,), (0,)), ((), ()))


def dot(a, b, dims=NN):
    return lax.dot_general(a, b, dims, preferred_element_type=F32)


def swap(block, bit):
    count = lax.axis_size("wide")
    return lax.ppermute(block, "wide", [(i, i ^ bit) for i in range(count)])


def after(value, *others):
    return lax.optimization_barrier((value, *others))[0]


def chip_gather(block, chips):
    if chips != 4:
        blocks, bit = [block], 1
        while bit < chips:
            blocks = blocks + [swap(b, 2 * bit) for b in blocks]
            bit *= 2
        return blocks
    half = block.shape[0] // 2
    top, low = block[:half], block[half:]
    top1, low2 = swap(top, 2), swap(low, 4)
    low1, top2 = swap(low, 2), swap(top, 4)
    top3, low3 = swap(top1, 4), swap(low2, 2)
    return [block, jnp.concatenate([top1, low1]), jnp.concatenate([top2, low2]), jnp.concatenate([top3, low3])]


def chip_scatter(parts, chips):
    if chips != 4:
        bit = chips // 2
        while bit:
            sums = [parts[r].astype(F32) + swap(parts[r + bit], 2 * bit).astype(F32) for r in range(bit)]
            parts = [total.astype(BF) for total in sums]
            bit //= 2
        return sums[0]
    half = parts[0].shape[0] // 2
    b = parts
    a2 = swap(b[3][:half], 2)
    c1 = swap(b[3][half:], 4)
    a0 = swap(b[1][:half], 2)
    c0 = swap(b[2][half:], 4)
    e0 = swap((b[2][:half].astype(F32) + a2.astype(F32)).astype(BF), 4)
    f0 = swap((b[1][half:].astype(F32) + c1.astype(F32)).astype(BF), 2)
    top = b[0][:half].astype(F32) + a0.astype(F32) + e0.astype(F32)
    low = b[0][half:].astype(F32) + c0.astype(F32) + f0.astype(F32)
    return jnp.concatenate([top, low])


def lanes_of(shape):
    return lax.broadcasted_iota(jnp.int32, shape, 1)


def turn(z, cos, sin):
    lane = lanes_of(z.shape) % HEAD_DIM
    other = jnp.where(lane < HEAD_DIM // 2, pltpu.roll(z, PAIR - HEAD_DIM // 2, 1), pltpu.roll(z, HEAD_DIM // 2, 1))
    return z * cos + other * sin


def both_heads(z):
    lane = lanes_of(z.shape)
    zero = jnp.zeros_like(z)
    return jnp.concatenate([jnp.where(lane < HEAD_DIM, z, zero), jnp.where(lane < HEAD_DIM, zero, z)], axis=0)


def join_heads(zt, size):
    row = lax.broadcasted_iota(jnp.int32, (PAIR, size), 0)
    return jnp.where(row < HEAD_DIM, zt[:, :size], zt[:, size:])


def open_keys(starts, first_key, size, diagonal):
    shape = (size, 2 * size)
    key = lax.broadcasted_iota(jnp.int32, shape, 0)
    allowed = key >= (starts - first_key)
    if diagonal:
        allowed = allowed & (key <= lanes_of(shape) % size)
    return allowed


def forward_kernel(size, first_ref, me_ref, q_ref, k_ref, v_ref, cos_ref, sin_ref, start_ref,
                   out_ref, qr_ref, kr_ref, vr_ref, lse_ref, vt, acc, top, total):
    blocks = q_ref.shape[0] // size
    me = me_ref[0]

    def rows_of(j):
        return pl.ds(pl.multiple_of(j * size, size), size)

    def prepare(j, _):
        rows = rows_of(j)
        cos, sin = cos_ref[rows, :], sin_ref[rows, :]
        qr_ref[rows, :] = (turn(q_ref[rows, :].astype(F32), cos, sin).astype(BF).astype(F32) * SCALE).astype(BF)
        kr_ref[rows, :] = turn(k_ref[rows, :].astype(F32), cos, sin).astype(BF)
        vt[:, rows] = jnp.transpose(v_ref[rows, :].astype(F32)).astype(BF)
        vr_ref[rows, :] = v_ref[rows, :]
        return 0

    lax.fori_loop(0, blocks, prepare, 0)

    def one_block(i, _):
        j = i ^ me
        rows = rows_of(j)
        q2 = both_heads(qr_ref[rows, :])
        start = start_ref[pl.ds(j, 1), :]
        starts = jnp.concatenate([start, start], axis=1)
        top[...] = jnp.full_like(top, NEG)
        total[...] = jnp.zeros_like(total)
        acc[...] = jnp.zeros_like(acc)

        def tile(b, diagonal):
            keys = rows_of(b ^ me)
            scores = dot(kr_ref[keys, :], q2, NT)
            scores = jnp.where(open_keys(starts, b * size, size, diagonal), scores, NEG)
            old = top[...]
            new = jnp.maximum(old, jnp.max(scores, axis=0, keepdims=True))
            probs = jnp.exp(scores - new)
            decay = jnp.exp(old - new)
            top[...] = new
            total[...] = total[...] * decay + jnp.sum(probs, axis=0, keepdims=True)
            acc[...] = acc[...] * decay + dot(vt[:, keys], probs.astype(BF))

        def body(b, _):
            tile(b, False)
            return 0

        lax.fori_loop(first_ref[i], i, body, 0)
        tile(i, True)
        scaled = acc[...] / total[...]
        out_ref[rows, :] = jnp.transpose(join_heads(scaled, size)).astype(BF)
        lse_ref[0, pl.ds(j, 1), :] = top[...] + jnp.log(total[...])
        return 0

    lax.fori_loop(0, blocks, one_block, 0)


def backward_kernel(size, first_ref, me_ref, q_ref, k_ref, v_ref, out_ref, do_ref, lse_ref, cos_ref, sin_ref,
                    start_ref, grad_ref, kt, dk, dv, dqt):
    blocks = q_ref.shape[0] // size
    me = me_ref[0]
    half = grad_ref.shape[1] // 3
    column = pl.program_id(1) * PAIR

    def rows_of(j):
        return pl.ds(pl.multiple_of(j * size, size), size)

    def place(which):
        return pl.ds(pl.multiple_of(which * half + column, PAIR), PAIR)

    def prepare(j, _):
        rows = rows_of(j)
        kt[:, rows] = jnp.transpose(k_ref[rows, :].astype(F32)).astype(BF)
        dk[rows, :] = jnp.zeros((size, PAIR), F32)
        dv[rows, :] = jnp.zeros((size, PAIR), F32)
        return 0

    lax.fori_loop(0, blocks, prepare, 0)

    def one_block(i, _):
        j = i ^ me
        rows = rows_of(j)
        q2 = both_heads(q_ref[rows, :])
        do = do_ref[rows, :]
        do2 = both_heads(do)
        start = start_ref[pl.ds(j, 1), :]
        starts = jnp.concatenate([start, start], axis=1)
        lse = lse_ref[0, pl.ds(j, 1), :]
        inner = jnp.transpose(do.astype(F32) * out_ref[rows, :].astype(F32))
        delta = jnp.concatenate([
            jnp.sum(inner[:HEAD_DIM], axis=0, keepdims=True),
            jnp.sum(inner[HEAD_DIM:], axis=0, keepdims=True),
        ], axis=1)
        dqt[...] = jnp.zeros_like(dqt)

        def tile(b, diagonal):
            keys = rows_of(b ^ me)
            scores = dot(k_ref[keys, :], q2, NT)
            allowed = open_keys(starts, b * size, size, diagonal)
            probs = jnp.where(allowed, jnp.exp(scores - lse), 0.0)
            dv[keys, :] += dot(probs.astype(BF), do2)
            dp = dot(v_ref[keys, :], do2, NT)
            ds = (probs * (dp - delta)).astype(BF)
            dk[keys, :] += dot(ds, q2)
            dqt[...] += dot(kt[:, keys], ds)

        def body(b, _):
            tile(b, False)
            return 0

        lax.fori_loop(first_ref[i], i, body, 0)
        tile(i, True)
        dq = jnp.transpose(join_heads(dqt[...], size)) * SCALE
        grad_ref[rows, place(0)] = turn(dq, cos_ref[rows, :], -sin_ref[rows, :]).astype(BF)
        return 0

    lax.fori_loop(0, blocks, one_block, 0)

    def finish(j, _):
        rows = rows_of(j)
        grad_ref[rows, place(1)] = turn(dk[rows, :], cos_ref[rows, :], -sin_ref[rows, :]).astype(BF)
        grad_ref[rows, place(2)] = dv[rows, :].astype(BF)
        return 0

    lax.fori_loop(0, blocks, finish, 0)


def attend(qkv, tables, size):
    seq, width = qkv.shape
    pairs = width // (3 * PAIR)
    per_half = pairs // 2
    first, me, cos, sin, starts = tables
    blocks = seq // size

    def take(which):
        return pl.BlockSpec((seq, PAIR), lambda h, w, *_: (0, (3 * h + which) * per_half + w))

    def whole(shape):
        return pl.BlockSpec(shape, lambda h, w, *_: (0, 0))

    mine = pl.BlockSpec((seq, PAIR), lambda h, w, *_: (0, h * per_half + w))
    return pl.pallas_call(
        functools.partial(forward_kernel, size),
        grid_spec=pltpu.PrefetchScalarGridSpec(
            num_scalar_prefetch=2,
            grid=(2, per_half),
            in_specs=[take(0), take(1), take(2), whole((seq, PAIR)), whole((seq, PAIR)), whole((blocks, size))],
            out_specs=[mine, mine, mine, mine, pl.BlockSpec((1, blocks, 2 * size), lambda h, w, *_: (h * per_half + w, 0, 0))],
            scratch_shapes=[
                pltpu.VMEM((PAIR, seq), BF),
                pltpu.VMEM((PAIR, 2 * size), F32),
                pltpu.VMEM((1, 2 * size), F32),
                pltpu.VMEM((1, 2 * size), F32),
            ],
        ),
        out_shape=[
            jax.ShapeDtypeStruct((seq, pairs * PAIR), BF),
            jax.ShapeDtypeStruct((seq, pairs * PAIR), BF),
            jax.ShapeDtypeStruct((seq, pairs * PAIR), BF),
            jax.ShapeDtypeStruct((seq, pairs * PAIR), BF),
            jax.ShapeDtypeStruct((pairs, blocks, 2 * size), F32),
        ],
        cost_estimate=pl.CostEstimate(flops=pairs * seq * seq * PAIR * 8, bytes_accessed=seq * width * 4,
                                      transcendentals=pairs * seq * seq // 2),
        name="attend_forward",
    )(first, me, qkv, qkv, qkv, cos, sin, starts)


def attend_back(qr, kr, vr, att, d_att, lse, tables, size):
    seq = qr.shape[0]
    pairs = qr.shape[1] // PAIR
    width = 3 * pairs * PAIR
    per_half = pairs // 2
    first, me, cos, sin, starts = tables
    blocks = seq // size
    mine = pl.BlockSpec((seq, PAIR), lambda h, w, *_: (0, h * per_half + w))

    def whole(shape):
        return pl.BlockSpec(shape, lambda h, w, *_: (0, 0))

    return pl.pallas_call(
        functools.partial(backward_kernel, size),
        grid_spec=pltpu.PrefetchScalarGridSpec(
            num_scalar_prefetch=2,
            grid=(2, per_half),
            in_specs=[
                mine, mine, mine, mine, mine,
                pl.BlockSpec((1, blocks, 2 * size), lambda h, w, *_: (h * per_half + w, 0, 0)),
                whole((seq, PAIR)), whole((seq, PAIR)), whole((blocks, size)),
            ],
            out_specs=pl.BlockSpec((seq, width // 2), lambda h, w, *_: (0, h)),
            scratch_shapes=[
                pltpu.VMEM((PAIR, seq), BF),
                pltpu.VMEM((seq, PAIR), F32),
                pltpu.VMEM((seq, PAIR), F32),
                pltpu.VMEM((PAIR, 2 * size), F32),
            ],
        ),
        out_shape=jax.ShapeDtypeStruct((seq, width), BF),
        cost_estimate=pl.CostEstimate(flops=pairs * seq * seq * PAIR * 20, bytes_accessed=seq * width * 8,
                                      transcendentals=pairs * seq * seq // 2),
        name="attend_backward",
    )(first, me, qr, kr, vr, att, d_att, lse, cos, sin, starts)


def norm_scale(values):
    return lax.rsqrt(jnp.mean(values * values, axis=-1, keepdims=True) + EPS)


def row_tables(lengths, me, size, seq):
    blocks = seq // size
    order = jnp.arange(blocks, dtype=jnp.int32) ^ me
    token = (order[:, None] * size + jnp.arange(size, dtype=jnp.int32)[None, :]).reshape(seq)
    ends = jnp.cumsum(lengths)

    def start_of(tokens):
        return jnp.max(jnp.where(ends[None, :] <= tokens[:, None], ends[None, :], jnp.int32(0)), axis=1)

    starts = start_of(token)
    first = start_of(jnp.arange(blocks, dtype=jnp.int32) * size) // size
    half = HEAD_DIM // 2
    inverse = ROPE_BASE ** (-(jnp.arange(half, dtype=F32) * 2.0) / HEAD_DIM)
    angles = (token - starts).astype(F32)[:, None] * inverse[None, :]
    cos, sin = jnp.cos(angles), jnp.sin(angles)
    return (
        first,
        me.reshape(1),
        jnp.concatenate([cos, cos, cos, cos], axis=1),
        jnp.concatenate([-sin, sin, -sin, sin], axis=1),
        starts.reshape(blocks, size),
    )


def per_device(hidden_in, out_grad, doc_lengths, attn_gain, w_query, w_key, w_value, w_out, mlp_gain, w_gate, w_up,
               w_down):
    wide = lax.axis_size("wide")
    narrow = lax.axis_size("narrow")
    chips = wide // 2
    me = lax.axis_index("wide")
    core = me % 2
    rows, size, dim = hidden_in.shape
    assert rows == 2
    seq = size * wide
    tokens = 2 * size

    def mine_of(both):
        keep = lax.dynamic_index_in_dim(both, core, 0, keepdims=False)
        send = lax.dynamic_index_in_dim(both, 1 - core, 0, keepdims=False)
        return jnp.concatenate([keep, swap(send, 1)])

    def rows_back(block):
        kept, got = block[:size], swap(block[size:], 1)
        return jnp.stack([jnp.where(core == 0, kept, got), jnp.where(core == 0, got, kept)])

    def fetch(shard):
        return lax.all_gather(shard, "narrow", axis=0, tiled=True)

    def rows_of(own):
        return jnp.concatenate([own, swap(own, 1)], axis=1)

    def columns_of(own):
        own = own.reshape(narrow, own.shape[0] // narrow, own.shape[1])
        return jnp.transpose(own, (1, 0, 2)).reshape(own.shape[1], dim)

    def share_rows(left, right):
        half = right.shape[1] // 2
        other = dot(left, right[:, half:], TN).astype(BF)
        own = dot(left, after(right, other)[:, :half], TN).astype(BF)
        total = (own.astype(F32) + swap(other, 1).astype(F32)).astype(BF)
        return lax.psum_scatter(total, "narrow", scatter_dimension=0, tiled=True), own

    def share_columns(grad):
        split = jnp.transpose(grad.reshape(grad.shape[0], narrow, dim // narrow), (1, 0, 2)).astype(BF)
        return lax.psum_scatter(split, "narrow", scatter_dimension=0, tiled=False)

    def block_of(array, r):
        return array[r * tokens:(r + 1) * tokens]

    gains = lax.all_gather(jnp.stack([attn_gain, mlp_gain]), "narrow", axis=1, tiled=True).astype(F32)
    attn_scale, mlp_scale = gains[0:1], gains[1:2]
    tables = row_tables(lax.dynamic_index_in_dim(doc_lengths, core, 0, keepdims=False), me, size, seq)

    own_qkv = fetch(jnp.concatenate([w_query, w_key, w_value], axis=1))
    own_out = fetch(after(w_out, own_qkv))
    own_gate = fetch(after(w_gate, own_out))
    own_up = fetch(after(w_up, own_gate))
    own_down = fetch(after(w_down, own_up))

    x_in = mine_of(hidden_in)
    x = x_in.astype(F32)
    r1 = norm_scale(x)
    u1 = x * r1
    attn_in = jnp.concatenate(chip_gather((u1 * attn_scale).astype(BF), chips))
    own_grad = mine_of(after(out_grad, x_in))
    w_qkv = rows_of(own_qkv)
    qkv = dot(attn_in, w_qkv).astype(BF)
    att, qr, kr, vr, lse = attend(qkv, tables, size)

    out_blocks = jnp.concatenate(chip_gather(columns_of(after(own_out, attn_in)), chips))
    full_out = jnp.concatenate([out_blocks, swap(out_blocks, 1)])
    grad_full = jnp.concatenate(chip_gather(after(own_grad, out_blocks), chips))
    width = att.shape[1]
    half = width // 2

    got = [block_of(att, 0)] + [swap(block_of(att, r), 2 * r) for r in range(1, chips)]
    att_full = jnp.concatenate([g[:, :half] for g in got] + [g[:, half:] for g in got], axis=1)
    middle = x + dot(att_full, full_out)
    r2 = norm_scale(middle)
    u2 = middle * r2
    mlp_in = jnp.concatenate(chip_gather((u2 * mlp_scale).astype(BF), chips))

    gate_w = rows_of(after(own_gate, att))
    up_w = rows_of(after(own_up, att))
    own_down = columns_of(own_down)
    down_w = jnp.concatenate([own_down, swap(own_down, 1)])

    gate_pre = dot(mlp_in, gate_w).astype(BF)
    up_pre = dot(mlp_in, after(up_w, gate_pre)).astype(BF)
    gate_f, up_f = gate_pre.astype(F32), up_pre.astype(F32)
    sigmoid = jax.nn.sigmoid(gate_f)
    silu = gate_f * sigmoid
    hidden = (silu * up_f).astype(BF)

    hidden_half = hidden.shape[1] // 2
    g_down = dot(hidden[:, hidden_half:], grad_full, TN).astype(BF)
    g_down_own = dot(after(hidden, g_down)[:, :hidden_half], grad_full, TN).astype(BF)
    grad_down = share_columns(g_down_own.astype(F32) + swap(g_down, 1).astype(F32))
    d_hidden = dot(grad_full, after(down_w, g_down_own), NT)
    d_gate = (d_hidden * up_f * sigmoid * (1.0 + gate_f * (1.0 - sigmoid))).astype(BF)
    d_up = (d_hidden * silu).astype(BF)

    d_parts = [None] * chips
    for r in reversed(range(chips)):
        d_parts[r] = (dot(block_of(d_gate, r), gate_w, NT) + dot(block_of(d_up, r), up_w, NT)).astype(BF)
    d_mlp = chip_scatter(d_parts, chips)
    grad_gate, g_gate = share_rows(mlp_in, after(d_gate, *d_parts))
    grad_up, g_up = share_rows(mlp_in, after(d_up, g_gate))

    d_mlp = after(d_mlp, g_up)
    e2 = d_mlp * mlp_scale
    gain_mlp = jnp.sum(d_mlp * u2, axis=0)
    d_mid = own_grad.astype(F32) + r2 * (e2 - u2 * jnp.mean(e2 * u2, axis=-1, keepdims=True))
    dm_b = d_mid.astype(BF)
    d_att_full = dot(dm_b, full_out, NT).astype(BF)

    def part(r, which):
        at = (which * chips + r) * half
        return d_att_full[:, at:at + half]

    sent = [jnp.concatenate([part(r, 0), part(r, 1)], axis=1) for r in range(chips)]
    d_att = jnp.concatenate([sent[0]] + [swap(sent[r], 2 * r) for r in range(1, chips)])
    g_out = dot(att_full, dm_b, TN).astype(BF)
    out_half = g_out.shape[0] // 2
    g_out = g_out[:out_half].astype(F32) + swap(g_out[out_half:], 1).astype(F32)

    out_parts = [dot(block_of(hidden, r), after(down_w, d_att_full)).astype(BF) for r in range(chips)]

    d_att, grad_down, g_out, *out_parts = lax.optimization_barrier((d_att, grad_down, g_out, *out_parts))
    output = middle + chip_scatter(out_parts, chips)
    out_rows = rows_back(output.astype(BF))
    d_qkv = attend_back(qr, kr, vr, att, d_att, lse, tables, size)
    d_qkv, grad_gate = lax.optimization_barrier((d_qkv, grad_gate))
    grad_out = share_columns(chip_scatter([g_out[r * half:(r + 1) * half].astype(BF) for r in range(chips)], chips))
    d_attn_parts = [None] * chips
    for r in reversed(range(chips)):
        d_attn_parts[r] = dot(block_of(d_qkv, r), w_qkv, NT).astype(BF)
    grad_qkv, _ = share_rows(attn_in, after(d_qkv, *d_attn_parts))
    grad_qkv = grad_qkv.astype(F32)
    d_attn = chip_scatter(d_attn_parts, chips)
    d_attn, grad_up, grad_out = lax.optimization_barrier((d_attn, grad_up, grad_out))
    u1 = after(x_in, d_attn).astype(F32) * r1
    e1 = d_attn * attn_scale
    gain_attn = jnp.sum(d_attn * u1, axis=0)
    in_grad = d_mid + r1 * (e1 - u1 * jnp.mean(e1 * u1, axis=-1, keepdims=True))
    in_rows = rows_back(in_grad.astype(BF))
    gain_grads = lax.psum_scatter(
        jnp.stack([gain_attn, gain_mlp]), ("narrow", "wide"), scatter_dimension=1, tiled=True
    )
    grad_out, grad_gate, grad_up, grad_down = (g.astype(F32) for g in (grad_out, grad_gate, grad_up, grad_down))
    return (
        out_rows,
        in_rows,
        gain_grads[0],
        grad_qkv[:, :half],
        grad_qkv[:, half:2 * half],
        grad_qkv[:, 2 * half:],
        grad_out,
        gain_grads[1],
        grad_gate,
        grad_up,
        grad_down,
    )


def solution(mesh):
    tokens, inner, outer = P("narrow", "wide", None), P("narrow", "wide"), P("wide", "narrow")
    gain_spec = P(("narrow", "wide"))
    in_specs = (
        tokens, tokens, P("narrow", None), P("narrow"), inner, inner, inner, outer, P("narrow"), inner, inner, outer,
    )
    out_specs = (tokens, tokens, gain_spec, inner, inner, inner, outer, gain_spec, inner, inner, outer)
    return jax.shard_map(per_device, mesh=mesh, in_specs=in_specs, out_specs=out_specs, check_vma=False)
```
